32 devices in a mesh: groups: 2 (over y), param: 4 (over z), walk: 4 (over x, core).
Axes of the slice: x: 2, y: 2, z: 4, core: 2. Of those that a mesh axis runs over, the one named last changes fastest.
Arguments:
- features: bfloat16 [8, 64, 64, 768], P(('groups', 'param'), 'walk'), parts along dimension 0, may hold values from -6 to 6
- occupancy: int32 [8, 64, 64], P(('groups', 'param'), 'walk'), parts along dimension 0, may hold values 0 or 1
- occ_embed: float32 [2, 768], replicated, may hold values from -6 to 6
- depth_kernel: bfloat16 [7, 7, 768], replicated, may hold values from -0.875 to 0.875
- up_weight: bfloat16 [768, 1536], P(None, 'param'), may hold values from -0.21875 to 0.21875
- down_weight_t: bfloat16 [768, 1536], P(None, 'param'), may hold values from -0.21875 to 0.21875
- cotangent: bfloat16 [8, 64, 64, 768], P(('groups', 'param'), 'walk'), parts along dimension 0, may hold values from -6 to 6
- a_inverse: float32 [768, 768], P('walk'), as said below
- g_inverse: float32 [1536, 1536], P(None, 'param'), as said below
Outputs:
- natural_grad: float32 [1536, 1536], P(('groups', 'walk'), 'param'), parts along dimension 0
The draws below stay inside these ranges and needn't reach their ends.
There are 2 independent parts, one for each index of `groups`. The reference program is written for one: setup_inputs(seed, part) draws one part's arguments, and reference() takes and returns one part's arrays. A program takes and returns all parts, laid end to end along the dimension named above; an argument that names none is the same for every part. Nothing has to cross between parts.
Inputs may be any that keep to these rules, and one draw needn't show every extreme that they name: `a_inverse`: a symmetric matrix. `g_inverse`: a symmetric matrix.
All inputs are finite; a program needn't handle non-finite values. No bound on the sum of `occupancy` on one device may be relied on, other than what follows from the above.
Results may differ from the reference program's by a relative error of at most 0.008.
Values may be sent and summed in bfloat16 or wider, within the bound.
No kernel may reach another device: no remote copies, remote signals or barrier semaphores. Data moves between devices by JAX's collectives and lax.ppermute only.
A program may use at most 64 MiB of HBM per device.

```python
import math
import jax
import jax.numpy as jnp
from jax import lax

D = 768
FF = 1536
LAT = 64
KS = 7
WALKERS = 4
N_WALK = 4


def build_inverse(off_diag, scales, order):
    symmetric = (off_diag + off_diag.T) * (0.3 / math.sqrt(order))
    core_matrix = jnp.eye(order, dtype=jnp.float32) + symmetric
    root_scale = jnp.sqrt(scales)
    return root_scale[:, None] * core_matrix * root_scale[None, :]


def draw_a_inverse(key, part):
    key_off, key_scale = jax.random.split(jax.random.fold_in(key, 11))
    off_diag = jax.random.normal(key_off, (D, D), jnp.float32)
    scales = jnp.exp(jax.random.uniform(key_scale, (D,), jnp.float32, 0.0, math.log(10.0)))
    return build_inverse(off_diag, scales, D)


def draw_g_inverse(key, part):
    key_off, key_scale = jax.random.split(jax.random.fold_in(key, 23))
    off_diag = jax.random.normal(key_off, (FF, FF), jnp.float32)
    scales = jnp.exp(jax.random.uniform(key_scale, (FF,), jnp.float32, 0.0, math.log(10.0)))
    return build_inverse(off_diag, scales, FF)


def place_ends(values, own_key, low, largest):
    index_at = [jax.random.randint(jax.random.fold_in(own_key, axis), (), 0, length) for axis, length in enumerate(values.shape)]
    longest = values.shape.index(max(values.shape))
    beside = index_at[:longest] + [(index_at[longest] + 1) % values.shape[longest]] + index_at[longest + 1:]
    return values.at[tuple(index_at)].set(low).at[tuple(beside)].set(largest)


def block_scale(rng, dims, cuts, smallest, top_value):
    loudness, own = 1.0, jax.random.fold_in(rng, 6)
    for dim, shards_of in cuts:
        draws = jnp.exp(jax.random.uniform(jax.random.fold_in(own, dim), (shards_of,), jnp.float32, smallest / len(cuts), top_value / len(cuts)))
        loudness = loudness * jnp.repeat(draws, dims[dim] // shards_of).reshape([-1 if axis == dim else 1 for axis in range(len(dims))])
    return loudness


def bell_draw(stream_key, dims, spread, most, pieces=(), held_as=jnp.bfloat16):
    drawn = jax.random.normal(stream_key, dims, jnp.float32) * spread
    if len(pieces) > 0:
        drawn = block_scale(stream_key, dims, pieces, -0.22, 0.18) * drawn
    return jnp.clip(drawn, min=-most, max=most).astype(held_as)


def setup_inputs(seed: int = 0, part: int = 0) -> dict:
    seeds = jax.random.split(jax.random.key(seed), 10)
    part_splits = jax.random.split(jax.random.fold_in(seeds[9], part), 10)
    features = bell_draw(part_splits[0], (WALKERS, LAT, LAT, D), 1.0, 6.0, ((0, 4), (1, 4)))
    occupancy = place_ends((jax.random.randint(part_splits[1], (WALKERS, LAT, LAT), 0, 2) < 1).astype(jnp.int32), jax.random.fold_in(part_splits[1], 1), 0, 1)
    occ_embed = bell_draw(seeds[2], (2, D), 1.0, 6.0, (), jnp.float32)
    depth_kernel = bell_draw(seeds[3], (KS, KS, D), (KS * KS) ** -0.5, 0.875)
    up_weight = bell_draw(seeds[4], (D, FF), D ** -0.5, 0.21875, ((1, 4),))
    down_weight_t = bell_draw(seeds[5], (D, FF), D ** -0.5, 0.21875, ((1, 4),))
    cotangent = bell_draw(part_splits[6], (WALKERS, LAT, LAT, D), 1.0, 6.0, ((0, 4), (1, 4)))
    a_inverse = draw_a_inverse(jax.random.fold_in(seeds[9], 71), part)
    g_inverse = draw_g_inverse(jax.random.fold_in(seeds[9], 71), part)
    return dict(features=features, occupancy=occupancy, occ_embed=occ_embed, depth_kernel=depth_kernel, up_weight=up_weight, down_weight_t=down_weight_t, cotangent=cotangent, a_inverse=a_inverse, g_inverse=g_inverse)


def gelu_slope(preact):
    cumulative = 0.5 * (1.0 + jax.scipy.special.erf(preact * 0.7071067811865476))
    density = jnp.exp(-0.5 * preact * preact) * 0.3989422804014327
    return cumulative + preact * density

def reference(features, occupancy, occ_embed, depth_kernel, up_weight, down_weight_t, cotangent, a_inverse, g_inverse):
    band_rows = LAT // N_WALK
    kernel_f = depth_kernel.astype(jnp.float32)

    def walker_step(running, walker_items):
        feature_grid, occupied, grad_out = walker_items
        embedded = jnp.where(occupied[..., None] == 1, occ_embed[1], occ_embed[0])
        stream = (feature_grid.astype(jnp.float32) + embedded).astype(jnp.bfloat16)
        stream_f = stream.astype(jnp.float32)
        mixed_sum = jnp.zeros((LAT, LAT, D), jnp.float32)
        for row_off in range(KS):
            for col_off in range(KS):
                mixed_sum = mixed_sum + kernel_f[row_off, col_off] * jnp.roll(stream_f, (3 - row_off, 3 - col_off), axis=(0, 1))
        mean_chan = lax.optimization_barrier(jnp.mean(mixed_sum, axis=-1, keepdims=True))
        centred = mixed_sum - mean_chan
        variance = lax.optimization_barrier(jnp.mean(centred * centred, axis=-1, keepdims=True))
        normed = (centred * lax.rsqrt(variance + 1e-06)).astype(jnp.bfloat16)
        tokens_flat = normed.reshape(LAT * LAT, D)
        grad_rows = grad_out.reshape(LAT * LAT, D)
        preact = jnp.dot(tokens_flat, up_weight, preferred_element_type=jnp.float32)
        back_hidden = jnp.dot(grad_rows, down_weight_t, preferred_element_type=jnp.float32)
        slopes = (back_hidden * gelu_slope(preact)).astype(jnp.bfloat16)
        band_tok = tokens_flat.reshape(N_WALK, band_rows * LAT, D).astype(jnp.float32)
        band_slope = slopes.reshape(N_WALK, band_rows * LAT, FF).astype(jnp.float32)
        band_parts = jnp.einsum('bkc,bkf->bcf', band_tok, band_slope).astype(jnp.bfloat16)
        band_parts = lax.optimization_barrier(band_parts).astype(jnp.float32)
        return (running + lax.optimization_barrier(jnp.sum(band_parts, axis=0)), None)
    running, _ = lax.scan(walker_step, jnp.zeros((D, FF), jnp.float32), (features, occupancy, cotangent))
    gradient = running / (LAT * LAT)
    left_part = jnp.dot(a_inverse, gradient, precision=lax.Precision.HIGHEST, preferred_element_type=jnp.float32)
    return jnp.dot(left_part, g_inverse, precision=lax.Precision.HIGHEST, preferred_element_type=jnp.float32)
```

```python
import functools

import jax
import jax.numpy as jnp
from jax import lax
from jax.experimental import pallas as pl
from jax.experimental.pallas import tpu as pltpu
from jax.sharding import PartitionSpec as P

LAT = 64
KS = 7
F32, BF16 = jnp.float32, jnp.bfloat16
NT = (((1,), (1,)), ((), ()))
NN = (((1,), (0,)), ((), ()))
TN = (((0,), (0,)), ((), ()))


def with_halo(value, sides, width):
    for axis, dim in sides:
        size, length = (lax.axis_size(axis), value.shape[dim])
        up = [(i, (i + 1) % size) for i in range(size)]
        down = [(j, i) for i, j in up]
        last = lax.slice_in_dim(value, length - width, length, axis=dim)
        first = lax.slice_in_dim(value, 0, width, axis=dim)
        before = lax.ppermute(last, axis, up)
        after = lax.ppermute(first, axis, down)
        value = jnp.concatenate([before, value, after], axis=dim)
    return value


def gelu_slope(preact):
    cumulative = 0.5 * (1.0 + jax.scipy.special.erf(preact * 0.7071067811865476))
    density = jnp.exp(-0.5 * preact * preact) * 0.3989422804014327
    return cumulative + preact * density


def general(
    features,
    occupancy,
    occ_embed,
    depth_kernel,
    up_weight,
    down_weight_t,
    cotangent,
    a_inverse,
    g_inverse,
):
    embedded = jnp.where(occupancy[..., None] == 1, occ_embed[1], occ_embed[0])
    stream = (features.astype(jnp.float32) + embedded).astype(jnp.bfloat16)
    padded = with_halo(stream, (("walk", 1),), 3)[0]
    padded = jnp.concatenate([padded[:, -3:], padded, padded[:, :3]], axis=1)
    row_count = stream.shape[1]
    col_count = stream.shape[2]
    channels = stream.shape[3]
    kernel_f = depth_kernel.astype(jnp.float32)
    mixed_sum = jnp.zeros((row_count, col_count, channels), jnp.float32)
    for row_off in range(KS):
        for col_off in range(KS):
            window = padded[row_off : row_off + row_count, col_off : col_off + col_count].astype(
                jnp.float32
            )
            mixed_sum = mixed_sum + kernel_f[row_off, col_off] * window
    mean_chan = jnp.mean(mixed_sum, axis=-1, keepdims=True)
    centred = mixed_sum - mean_chan
    variance = jnp.mean(centred * centred, axis=-1, keepdims=True)
    normed = (
        (centred * lax.rsqrt(variance + 1e-06))
        .astype(jnp.bfloat16)
        .reshape(row_count * col_count, channels)
    )
    grad_rows = cotangent.reshape(row_count * col_count, channels)
    up_full, down_full = (
        lax.all_gather(up_weight, "param", axis=1, tiled=True),
        lax.all_gather(down_weight_t, "param", axis=1, tiled=True),
    )
    preact = jnp.dot(normed, up_full, preferred_element_type=jnp.float32)
    back_hidden = jnp.dot(grad_rows, down_full, preferred_element_type=jnp.float32)
    slopes = (back_hidden * gelu_slope(preact)).astype(jnp.bfloat16)
    owned_rows = lax.psum_scatter(
        lax.dot_general(
            normed, slopes, (((0,), (0,)), ((), ())), preferred_element_type=jnp.float32
        ).astype(jnp.bfloat16),
        "walk",
        scatter_dimension=0,
        tiled=True,
    ).astype(jnp.float32)
    owned_sum = lax.psum_scatter(owned_rows, "param", scatter_dimension=1, tiled=True) / (LAT * LAT)
    left_part = jnp.dot(
        a_inverse,
        lax.all_gather(owned_sum, "walk", axis=0, tiled=True),
        precision=lax.Precision.HIGHEST,
        preferred_element_type=jnp.float32,
    )
    return jnp.dot(
        lax.all_gather(left_part, "param", axis=1, tiled=True),
        g_inverse,
        precision=lax.Precision.HIGHEST,
        preferred_element_type=jnp.float32,
    )


def matmul(a, b, dims):
    return lax.dot_general(a, b, dims, preferred_element_type=F32)


def conv_body(feat_ref, occ_ref, emb_ref, top_ref, bot_ref, ker_ref, out_ref, grid_ref, tap_ref, mix_ref):
    rows, cols, chans = feat_ref.shape
    half = KS // 2
    blocks = chans // 128
    pitch = cols + 16
    for t in range(KS * KS):
        for b in range(blocks):
            tap_ref[b, t] = jnp.broadcast_to(ker_ref[t : t + 1, b * 128 : (b + 1) * 128], (8, 128))

    def put(slot, value):
        base = slot * pitch + 8
        for b in range(blocks):
            part = value[:, b * 128 : (b + 1) * 128]
            grid_ref[b, base : base + cols, :] = part
            grid_ref[b, base - half : base, :] = part[cols - half :]
            grid_ref[b, base + cols : base + cols + half, :] = part[:half]

    for i in range(half):
        put(i, top_ref[i].astype(F32))
        put(half + rows + i, bot_ref[i].astype(F32))
    low = emb_ref[0:1, :]
    high = emb_ref[1:2, :]
    for i in range(rows):
        on = occ_ref[:, i : i + 1] == 1
        value = feat_ref[i].astype(F32) + jnp.where(on, high, low)
        put(half + i, value.astype(BF16).astype(F32))
    groups = cols // 8

    def convolve(n, carry):
        b = n // groups
        j = pl.multiple_of((n % groups) * 8, 8)
        acc = [jnp.zeros((8, 128), F32) for _ in range(rows)]
        for s in range(KS):
            taps = [tap_ref[b, r * KS + s] for r in range(KS)]
            for i in range(rows + 2 * half):
                x = grid_ref[b, pl.ds(j + (i * pitch + 8 - half + s), 8), :]
                for r in range(KS):
                    if 0 <= i - r < rows:
                        acc[i - r] = acc[i - r] + taps[r] * x
        for o in range(rows):
            mix_ref[b, pl.ds(j + o * cols, 8), :] = acc[o]
        return carry

    lax.fori_loop(0, blocks * groups, convolve, 0)
    span = 32

    def normalise(n, carry):
        at = pl.multiple_of(n * span, span)
        parts = [mix_ref[b, pl.ds(at, span), :] for b in range(blocks)]
        mean = jnp.sum(functools.reduce(jnp.add, parts), axis=-1, keepdims=True) * (1.0 / chans)
        parts = [p - mean for p in parts]
        squares = functools.reduce(jnp.add, [p * p for p in parts])
        scale = lax.rsqrt(jnp.sum(squares, axis=-1, keepdims=True) * (1.0 / chans) + 1e-06)
        for b in range(blocks):
            out_ref[pl.ds(at, span), b * 128 : (b + 1) * 128] = (parts[b] * scale).astype(BF16)
        return carry

    lax.fori_loop(0, rows * cols // span, normalise, 0, unroll=4)


def conv_norm(feat, occ_cols, emb, top, bottom, kernel):
    rows, cols, chans = feat.shape
    blocks = chans // 128
    return pl.pallas_call(
        conv_body,
        out_shape=jax.ShapeDtypeStruct((rows * cols, chans), BF16),
        in_specs=[pl.BlockSpec(memory_space=pltpu.VMEM)] * 6,
        out_specs=pl.BlockSpec(memory_space=pltpu.VMEM),
        scratch_shapes=[
            pltpu.VMEM((blocks, (rows + KS - 1) * (cols + 16), 128), F32),
            pltpu.VMEM((blocks, KS * KS, 8, 128), F32),
            pltpu.VMEM((blocks, rows * cols, 128), F32),
        ],
        compiler_params=pltpu.CompilerParams(vmem_limit_bytes=24 * 1024 * 1024),
        cost_estimate=pl.CostEstimate(
            flops=2 * KS * KS * feat.size, transcendentals=0, bytes_accessed=4 * feat.size
        ),
        name="conv_norm",
    )(feat, occ_cols, emb, top, bottom, kernel)


def gelu_slope_in(x):
    cumulative = 0.5 * (1.0 + lax.erf(x * 0.7071067811865476))
    density = jnp.exp(-0.5 * x * x) * 0.3989422804014327
    return cumulative + x * density


def chunk_body(n0, n1, c0, c1, w0, w1, mine_hi, mine_lo, other_hi, other_lo, keep_ref, send_ref, acc_ref):
    half = w0.shape[0] // 2
    up = jnp.concatenate([w0[:half], w1[:half]], axis=0)
    down = jnp.concatenate([w0[half:], w1[half:]], axis=0)
    block = 512
    first = True
    for n_ref, c_ref in ((n0, c0), (n1, c1)):
        for at in range(0, n_ref.shape[0], block):
            normed = n_ref[at : at + block]
            pre = matmul(up, normed, NT)
            back = matmul(down, c_ref[at : at + block], NT)
            slopes = (back * gelu_slope_in(pre)).astype(BF16)
            part = matmul(slopes, normed, NN)
            acc_ref[...] = part if first else acc_ref[...] + part
            first = False
    summed = acc_ref[...].astype(BF16)
    keep_ref[...] = matmul(summed, mine_hi[...], NT) + matmul(summed, mine_lo[...], NT)
    send_ref[...] = (matmul(summed, other_hi[...], NT) + matmul(summed, other_lo[...], NT)).astype(BF16)


def chunk(sites, weights, mine, other):
    hidden, chans = weights[0].shape
    rows = mine[0].shape[0]
    count = 2 * sites[0].shape[0]
    return pl.pallas_call(
        chunk_body,
        out_shape=(
            jax.ShapeDtypeStruct((hidden, rows), F32),
            jax.ShapeDtypeStruct((hidden, rows), BF16),
        ),
        in_specs=[pl.BlockSpec(memory_space=pltpu.VMEM)] * 10,
        out_specs=(pl.BlockSpec(memory_space=pltpu.VMEM),) * 2,
        scratch_shapes=[pltpu.VMEM((hidden, chans), F32)],
        compiler_params=pltpu.CompilerParams(vmem_limit_bytes=24 * 1024 * 1024),
        cost_estimate=pl.CostEstimate(
            flops=6 * count * hidden * chans, transcendentals=0, bytes_accessed=4 * count * chans
        ),
        name="chunk",
    )(*sites, *weights, *mine, *other)


def split(value):
    high = lax.reduce_precision(value, 8, 7)
    return high.astype(BF16), (value - high).astype(BF16)


def flip(value, axis, bit):
    size = lax.axis_size(axis)
    return lax.ppermute(value, axis, [(i, i ^ bit) for i in range(size)])


def paired(
    features,
    occupancy,
    occ_embed,
    depth_kernel,
    up_weight,
    down_weight_t,
    cotangent,
    a_inverse,
    g_inverse,
):
    _, rows, cols, chans = features.shape
    sites = rows * cols
    planes = lax.axis_size("param")
    half = KS // 2
    core = lax.axis_index("walk") % 2
    group = lax.axis_index("groups")
    plane = lax.axis_index("param")

    def embed(part, occupied):
        embedded = jnp.where(occupied[..., None] == 1, occ_embed[1], occ_embed[0])
        return (part.astype(F32) + embedded).astype(BF16)

    grid, occupied = features[0], occupancy[0]
    ring = [(i, (i + 1) % lax.axis_size("walk")) for i in range(lax.axis_size("walk"))]
    first = embed(grid[:half], occupied[:half])
    last = embed(grid[rows - half :], occupied[rows - half :])
    top = lax.ppermute(last, "walk", ring)
    bottom = lax.ppermute(first, "walk", [(j, i) for i, j in ring])

    width = up_weight.shape[1]
    piece = width // 4
    pieces = [
        lax.dynamic_index_in_dim(w.T.reshape(2, 2, piece, chans), core, 0, keepdims=False)
        for w in (up_weight, down_weight_t)
    ]

    def of_group(which):
        picked = [lax.dynamic_index_in_dim(p, which, 0, keepdims=False) for p in pieces]
        return jnp.concatenate(picked, axis=0)

    weights = [(of_group(group), of_group(1 - group))]
    for k in range(1, planes):
        mine = flip(weights[0][0], "param", k)
        weights.append((mine, flip(mine, "groups", 1)))

    grads = cotangent[0].reshape(sites, chans)
    grads_pair = flip(grads, "walk", 1)
    across = flip(a_inverse, "walk", 2)
    stacked = jnp.concatenate([a_inverse, across], axis=0)
    stacked_pair = flip(stacked, "walk", 1)
    share = a_inverse.shape[0]
    mine = split(jnp.concatenate([a_inverse, stacked_pair[:share]], axis=0))
    other = split(jnp.concatenate([across, stacked_pair[share:]], axis=0))

    normed = conv_norm(
        grid, occupied.T, occ_embed, top, bottom, depth_kernel.reshape(KS * KS, chans).astype(F32)
    )
    normed_pair = flip(normed, "walk", 1)

    owned = None
    for k in range(planes):
        keep, send = chunk((normed, normed_pair, grads, grads_pair), weights[k], mine, other)
        total = keep + flip(send, "walk", 2).astype(F32)
        if k > 0:
            total = flip(total.astype(BF16), "param", k).astype(F32)
        owned = total if owned is None else owned + total
    left = owned.astype(BF16)

    g_rows = g_inverse.reshape(planes, 2, 2, piece, width)
    result = None
    for k in range(planes):
        block = lax.dynamic_index_in_dim(g_rows, plane ^ k, 0, keepdims=False)
        block = lax.dynamic_index_in_dim(block, core, 0, keepdims=False)
        block = jnp.where(group == 0, block, block[::-1]).reshape(2 * piece, width)
        high, low = split(block)
        part = left if k == 0 else flip(left, "param", k)
        term = matmul(part, high, TN) + matmul(part, low, TN)
        result = term if result is None else result + term
    result = result * (1.0 / (LAT * LAT))
    return result[:share] + flip(result[share:], "walk", 1)


def solution(mesh):
    sizes = mesh.shape
    pairs = sizes["walk"] == 4 and sizes["groups"] == 2 and sizes["param"] in (2, 4, 8)
    placed = (
        P(("groups", "param"), "walk", None, None),
        P(("groups", "param"), "walk", None),
        P(),
        P(),
        P(None, "param"),
        P(None, "param"),
        P(("groups", "param"), "walk", None, None),
        P("walk", None),
        P(None, "param"),
    )
    return jax.shard_map(
        paired if pairs else general,
        mesh=mesh,
        in_specs=placed,
        out_specs=P(("groups", "walk"), "param"),
        check_vma=False,
    )
```

```python
import functools

import jax
import jax.numpy as jnp
from jax import lax
from jax.experimental import pallas as pl
from jax.experimental.pallas import tpu as pltpu
from jax.sharding import PartitionSpec as P


LAT = 64
KS = 7
F32, BF16 = jnp.float32, jnp.bfloat16
NT = (((1,), (1,)), ((), ()))
NN = (((1,), (0,)), ((), ()))
TN = (((0,), (0,)), ((), ()))


def with_halo(value, sides, width):
    for axis, dim in sides:
        size, length = (lax.axis_size(axis), value.shape[dim])
        up = [(i, (i + 1) % size) for i in range(size)]
        down = [(j, i) for i, j in up]
        last = lax.slice_in_dim(value, length - width, length, axis=dim)
        first = lax.slice_in_dim(value, 0, width, axis=dim)
        before = lax.ppermute(last, axis, up)
        after = lax.ppermute(first, axis, down)
        value = jnp.concatenate([before, value, after], axis=dim)
    return value


def gelu_slope(preact):
    cumulative = 0.5 * (1.0 + jax.scipy.special.erf(preact * 0.7071067811865476))
    density = jnp.exp(-0.5 * preact * preact) * 0.3989422804014327
    return cumulative + preact * density


def general(
    features,
    occupancy,
    occ_embed,
    depth_kernel,
    up_weight,
    down_weight_t,
    cotangent,
    a_inverse,
    g_inverse,
):
    embedded = jnp.where(occupancy[..., None] == 1, occ_embed[1], occ_embed[0])
    stream = (features.astype(jnp.float32) + embedded).astype(jnp.bfloat16)
    padded = with_halo(stream, (("walk", 1),), 3)[0]
    padded = jnp.concatenate([padded[:, -3:], padded, padded[:, :3]], axis=1)
    row_count = stream.shape[1]
    col_count = stream.shape[2]
    channels = stream.shape[3]
    kernel_f = depth_kernel.astype(jnp.float32)
    mixed_sum = jnp.zeros((row_count, col_count, channels), jnp.float32)
    for row_off in range(KS):
        for col_off in range(KS):
            window = padded[row_off : row_off + row_count, col_off : col_off + col_count].astype(
                jnp.float32
            )
            mixed_sum = mixed_sum + kernel_f[row_off, col_off] * window
    mean_chan = jnp.mean(mixed_sum, axis=-1, keepdims=True)
    centred = mixed_sum - mean_chan
    variance = jnp.mean(centred * centred, axis=-1, keepdims=True)
    normed = (
        (centred * lax.rsqrt(variance + 1e-06))
        .astype(jnp.bfloat16)
        .reshape(row_count * col_count, channels)
    )
    grad_rows = cotangent.reshape(row_count * col_count, channels)
    up_full, down_full = (
        lax.all_gather(up_weight, "param", axis=1, tiled=True),
        lax.all_gather(down_weight_t, "param", axis=1, tiled=True),
    )
    preact = jnp.dot(normed, up_full, preferred_element_type=jnp.float32)
    back_hidden = jnp.dot(grad_rows, down_full, preferred_element_type=jnp.float32)
    slopes = (back_hidden * gelu_slope(preact)).astype(jnp.bfloat16)
    owned_rows = lax.psum_scatter(
        lax.dot_general(
            normed, slopes, (((0,), (0,)), ((), ())), preferred_element_type=jnp.float32
        ).astype(jnp.bfloat16),
        "walk",
        scatter_dimension=0,
        tiled=True,
    ).astype(jnp.float32)
    owned_sum = lax.psum_scatter(owned_rows, "param", scatter_dimension=1, tiled=True) / (LAT * LAT)
    left_part = jnp.dot(
        a_inverse,
        lax.all_gather(owned_sum, "walk", axis=0, tiled=True),
        precision=lax.Precision.HIGHEST,
        preferred_element_type=jnp.float32,
    )
    return jnp.dot(
        lax.all_gather(left_part, "param", axis=1, tiled=True),
        g_inverse,
        precision=lax.Precision.HIGHEST,
        preferred_element_type=jnp.float32,
    )


def matmul(a, b, dims):
    return lax.dot_general(a, b, dims, preferred_element_type=F32)


def conv_body(plan, inner, feat_ref, occ_ref, emb_ref, *refs):
    if inner:
        ker_ref, out_ref, grid_ref, tap_ref, mix_ref = refs
    else:
        top_ref, bot_ref, mid_ref, ker_ref, out_ref, grid_ref, tap_ref, mix_ref = refs
    rows, cols, chans = feat_ref.shape
    slots, runs = plan
    half = KS // 2
    blocks = chans // 128
    pitch = cols + 16
    for t in range(KS * KS):
        for b in range(blocks):
            tap_ref[b, t] = jnp.broadcast_to(ker_ref[t : t + 1, b * 128 : (b + 1) * 128], (8, 128))
    low = emb_ref[0:1, :]
    high = emb_ref[1:2, :]
    for slot, row in enumerate(slots):
        if row < 0:
            value = top_ref[row + half].astype(F32)
        elif row >= rows:
            value = bot_ref[row - rows].astype(F32)
        else:
            on = occ_ref[:, row : row + 1] == 1
            value = feat_ref[row].astype(F32) + jnp.where(on, high, low)
            value = value.astype(BF16).astype(F32)
        base = slot * pitch + 8
        for b in range(blocks):
            part = value[:, b * 128 : (b + 1) * 128]
            grid_ref[b, base : base + cols, :] = part
            grid_ref[b, base - half : base, :] = part[cols - half :]
            grid_ref[b, base + cols : base + cols + half, :] = part[:half]
    groups = cols // 8

    def convolve(n, carry):
        b = n // groups
        j = pl.multiple_of((n % groups) * 8, 8)
        done = 0
        for start, count in runs:
            acc = [jnp.zeros((8, 128), F32) for _ in range(count)]
            for s in range(KS):
                taps = [tap_ref[b, r * KS + s] for r in range(KS)]
                for i in range(count + KS - 1):
                    x = grid_ref[b, pl.ds(j + ((start + i) * pitch + 8 - half + s), 8), :]
                    for r in range(KS):
                        if 0 <= i - r < count:
                            acc[i - r] = acc[i - r] + taps[r] * x
            for o in range(count):
                mix_ref[b, pl.ds(j + (done + o) * cols, 8), :] = acc[o]
            done += count
        return carry

    lax.fori_loop(0, blocks * groups, convolve, 0)
    span = 32
    edge, skip = mix_ref.shape[1], 0
    if not inner:
        edge, skip = runs[0][1] * cols, mid_ref.shape[0]
        out_ref[edge : edge + skip] = mid_ref[...]

    def normalise(n, carry):
        at = pl.multiple_of(n * span, span)
        parts = [mix_ref[b, pl.ds(at, span), :] for b in range(blocks)]
        mean = jnp.sum(functools.reduce(jnp.add, parts), axis=-1, keepdims=True) * (1.0 / chans)
        parts = [p - mean for p in parts]
        squares = functools.reduce(jnp.add, [p * p for p in parts])
        scale = lax.rsqrt(jnp.sum(squares, axis=-1, keepdims=True) * (1.0 / chans) + 1e-06)
        to = pl.multiple_of(at + jnp.where(at >= edge, skip, 0), span)
        for b in range(blocks):
            out_ref[pl.ds(to, span), b * 128 : (b + 1) * 128] = (parts[b] * scale).astype(BF16)
        return carry

    lax.fori_loop(0, mix_ref.shape[1] // span, normalise, 0, unroll=4)


def conv_norm(feat, occ_cols, emb, kernel, edges=None):
    rows, cols, chans = feat.shape
    blocks = chans // 128
    half = KS // 2
    quarter = rows // 4
    if edges is None:
        slots = tuple(range(quarter - half, rows - quarter + half))
        runs = ((0, rows - 2 * quarter),)
        args = (feat, occ_cols, emb, kernel)
    else:
        slots = tuple(range(-half, quarter + half)) + tuple(range(rows - quarter - half, rows + half))
        runs = ((0, quarter), (quarter + 2 * half, quarter))
        args = (feat, occ_cols, emb, *edges, kernel)
    count = sum(r for _, r in runs) * cols
    return pl.pallas_call(
        functools.partial(conv_body, (slots, runs), edges is None),
        out_shape=jax.ShapeDtypeStruct((count if edges is None else rows * cols, chans), BF16),
        in_specs=[pl.BlockSpec(memory_space=pltpu.VMEM)] * len(args),
        out_specs=pl.BlockSpec(memory_space=pltpu.VMEM),
        scratch_shapes=[
            pltpu.VMEM((blocks, len(slots) * (cols + 16), 128), F32),
            pltpu.VMEM((blocks, KS * KS, 8, 128), F32),
            pltpu.VMEM((blocks, count, 128), F32),
        ],
        compiler_params=pltpu.CompilerParams(vmem_limit_bytes=12 * 1024 * 1024),
        cost_estimate=pl.CostEstimate(
            flops=2 * KS * KS * feat.size, transcendentals=0, bytes_accessed=4 * feat.size
        ),
        name="conv_inner" if edges is None else "conv_outer",
    )(*args)


def gelu_slope_in(x):
    cumulative = 0.5 * (1.0 + lax.erf(x * 0.7071067811865476))
    density = jnp.exp(-0.5 * x * x) * 0.3989422804014327
    return cumulative + x * density


def chunk_body(n0, n1, c0, c1, w0, w1, mine, other, keep_ref, send_ref, acc_ref):
    half = w0.shape[0] // 2
    up = jnp.concatenate([w0[:half], w1[:half]], axis=0)
    down = jnp.concatenate([w0[half:], w1[half:]], axis=0)
    block = n0.shape[0] // 2
    first = True
    for n_ref, c_ref in ((n0, c0), (n1, c1)):
        for at in (0, block):
            normed = n_ref[at : at + block]
            pre = matmul(up, normed, NT)
            back = matmul(down, c_ref[at : at + block], NT)
            slopes = (back * gelu_slope_in(pre)).astype(BF16)
            part = matmul(slopes, normed, NN)
            acc_ref[...] = part if first else acc_ref[...] + part
            first = False
    summed = acc_ref[...].astype(BF16)
    send_ref[...] = matmul(summed, other[...], NT).astype(BF16)
    keep_ref[...] = matmul(summed, mine[...], NT)


def chunk(sites, weights, inverse):
    hidden, chans = weights[0].shape
    rows = inverse[0].shape[0]
    count = 2 * sites[0].shape[0]
    return pl.pallas_call(
        chunk_body,
        out_shape=(
            jax.ShapeDtypeStruct((hidden, rows), F32),
            jax.ShapeDtypeStruct((hidden, rows), BF16),
        ),
        in_specs=[pl.BlockSpec(memory_space=pltpu.VMEM)] * 8,
        out_specs=(pl.BlockSpec(memory_space=pltpu.VMEM),) * 2,
        scratch_shapes=[pltpu.VMEM((hidden, chans), F32)],
        compiler_params=pltpu.CompilerParams(vmem_limit_bytes=12 * 1024 * 1024),
        cost_estimate=pl.CostEstimate(
            flops=6 * count * hidden * chans, transcendentals=0, bytes_accessed=4 * count * chans
        ),
        name="chunk",
    )(*sites, *weights, *inverse)


def split(value):
    high = lax.reduce_precision(value, 8, 7)
    return high.astype(BF16), (value - high).astype(BF16)


def flip(value, axis, bit):
    size = lax.axis_size(axis)
    return lax.ppermute(value, axis, [(i, i ^ bit) for i in range(size)])


def after(value, *others):
    return lax.optimization_barrier((value, *others))[0]


def paired(
    features,
    occupancy,
    occ_embed,
    depth_kernel,
    up_weight,
    down_weight_t,
    cotangent,
    a_inverse,
    g_inverse,
):
    _, rows, cols, chans = features.shape
    sites = rows * cols
    planes = lax.axis_size("param")
    half = KS // 2
    core = lax.axis_index("walk") % 2
    group = lax.axis_index("groups")
    plane = lax.axis_index("param")

    width = up_weight.shape[1]
    piece = width // 4
    pieces = [
        lax.dynamic_index_in_dim(w.T.reshape(2, 2, piece, chans), core, 0, keepdims=False)
        for w in (up_weight, down_weight_t)
    ]

    def of_group(which):
        picked = [lax.dynamic_index_in_dim(p, which, 0, keepdims=False) for p in pieces]
        return jnp.concatenate(picked, axis=0)

    local = of_group(group)
    near = {k: flip(local, "param", k) for k in range(1, min(3, planes))}

    def embed(part, occupied):
        embedded = jnp.where(occupied[..., None] == 1, occ_embed[1], occ_embed[0])
        return (part.astype(F32) + embedded).astype(BF16)

    grid, occupied = features[0], occupancy[0]
    ring = [(i, (i + 1) % lax.axis_size("walk")) for i in range(lax.axis_size("walk"))]
    first = embed(grid[:half], occupied[:half])
    last = embed(grid[rows - half :], occupied[rows - half :])
    top = lax.ppermute(last, "walk", ring)
    bottom = lax.ppermute(first, "walk", [(j, i) for i, j in ring])

    taps = depth_kernel.reshape(KS * KS, chans).astype(F32)
    columns = occupied.T
    inner = conv_norm(grid, columns, occ_embed, taps)
    distant = dict(near)
    for k in range(3, planes):
        distant[k] = flip(after(local, inner, *near.values()), "param", k)

    grads = cotangent[0].reshape(sites, chans)
    grads_pair = flip(grads, "walk", 1)
    share = a_inverse.shape[0]
    inverse = a_inverse.astype(BF16)
    across = flip(after(inverse, inner), "walk", 2)
    beside = flip(inverse, "walk", 1)

    outer = conv_norm(after(grid, inner, *near.values()), columns, occ_embed, taps, (top, bottom, inner))
    normed_pair = flip(outer, "walk", 1)
    diagonal = flip(across, "walk", 1)
    inverse = (
        jnp.concatenate([after(inverse, outer), beside], axis=0),
        jnp.concatenate([after(across, outer), diagonal], axis=0),
    )

    weights = {k: (w, flip(w, "groups", 1)) for k, w in distant.items()}
    weights[0] = (local, of_group(1 - group))
    order = (*range(2, planes), 1, 0)
    operands = (outer, normed_pair, grads, grads_pair)
    owned = None
    history = []
    for k in order:
        earlier = [keep for keep, _ in history[-1:]] + [total for _, total in history[:-1]]
        pair = weights[k]
        if earlier:
            pair = (after(pair[0], *earlier), pair[1])
        keep, send = chunk(operands, pair, inverse)
        total = keep + flip(send, "walk", 2).astype(F32)
        history.append((keep, total))
        if k > 0:
            total = flip(total.astype(BF16), "param", k).astype(F32)
        owned = total if owned is None else owned + total
    ours, theirs = owned[:, :share].astype(BF16), owned[:, share:].astype(BF16)
    left = jnp.concatenate([ours, flip(theirs, "walk", 1)], axis=1)

    g_rows = after(g_inverse, left).reshape(planes, 2, 2, piece, width)
    parts = [left] + [flip(left, "param", k) for k in range(1, planes)]
    result = None
    for k, part in enumerate(parts):
        block = lax.dynamic_index_in_dim(g_rows, plane ^ k, 0, keepdims=False)
        block = jnp.where(group == 0, block, block[:, ::-1])
        block = jnp.where(core == 0, block, block[::-1]).reshape(2, 2 * piece, width)
        high, low = split(block)
        for c in range(2):
            rows_t = part[:, c * share : (c + 1) * share]
            term = matmul(rows_t, high[c], TN) + matmul(rows_t, low[c], TN)
            result = term if result is None else result + term
    return result * (1.0 / (LAT * LAT))


def solution(mesh):
    sizes = mesh.shape
    pairs = sizes["walk"] == 4 and sizes["groups"] == 2 and sizes["param"] in (2, 4, 8)
    placed = (
        P(("groups", "param"), "walk", None, None),
        P(("groups", "param"), "walk", None),
        P(),
        P(),
        P(None, "param"),
        P(None, "param"),
        P(("groups", "param"), "walk", None, None),
        P("walk", None),
        P(None, "param"),
    )

    def staged(*arrays):
        return paired(*arrays)

    return jax.shard_map(
        staged if pairs else general,
        mesh=mesh,
        in_specs=placed,
        out_specs=P(("groups", "walk"), "param"),
        check_vma=False,
    )
```
